32 devices in a mesh: tm: 8 (over y, x, core), floor: 4 (over z).
Axes of the slice: x: 2, y: 2, z: 4, core: 2. Of those that a mesh axis runs over, the one named last changes fastest.
Arguments:
- samples: bfloat16 [8, 16, 32768], P('tm', None, 'floor'), may hold values from -6 to 6
- operator: bfloat16 [8, 512, 32768], P('tm', None, 'floor'), may hold values from -0.01171875 to 0.01171875
Outputs:
- sensor_data: bfloat16 [8, 16, 512], P('tm', None, 'floor')
The draws below stay inside these ranges and needn't reach their ends.
All inputs are finite; a program needn't handle non-finite values.
Results may differ from the reference program's by a relative error of at most 0.0013.
Values may be sent and summed in bfloat16 or wider, within the bound.
A program may use at most 64 MiB of HBM per device.

```python
import jax
import jax.numpy as jnp
from jax import lax

S = 512
P_SIZE = 32768
K = 16
NT = 8


def level_of(key, shape, cuts, low, high):
    def one(dim, parts):
        heights = jax.random.uniform(jax.random.fold_in(jax.random.fold_in(key, 6), dim), (parts,), jnp.float32, low / len(cuts), high / len(cuts))
        return jnp.repeat(jnp.exp(heights), shape[dim] // parts).reshape((-1,) + (1,) * (len(shape) - dim - 1))

    factor_of = one(*cuts[0])
    for cut in cuts[1:]:
        factor_of = factor_of * one(*cut)
    return factor_of


def noise(rng, dims, width, bound, pieces=(), kind=jnp.bfloat16):
    result = jax.random.normal(rng, dims, jnp.float32) * width
    if len(pieces) > 0:
        result = level_of(rng, dims, pieces, -0.22, 0.18) * result
    return jnp.clip(result, min=-bound, max=bound).astype(kind)


def setup_inputs(seed: int = 0) -> dict:
    splits = jax.random.split(jax.random.key(seed), 3)
    return {
        "samples": noise(splits[0], (NT, K, P_SIZE), 1.0, 6.0, ((0, 8), (2, 4))),
        "operator": noise(splits[1], (NT, S, P_SIZE), (P_SIZE * NT) ** -0.5, 0.01171875, ((0, 8), (2, 4))),
    }


def reference(samples, operator):
    blocks = samples.astype(jnp.float32)

    def add_lag(total, lag):
        kernel = lax.dynamic_index_in_dim(operator, lag, 0, keepdims=False).astype(jnp.float32)
        images = jnp.einsum('tki,si->tks', blocks, kernel)
        padded = jnp.pad(images, ((NT, 0), (0, 0), (0, 0)))
        shifted = lax.dynamic_slice_in_dim(padded, (NT - lag).astype(jnp.int32), NT, 0)
        return total + shifted, None

    start = jnp.zeros((NT, K, S), jnp.float32)
    total, _ = lax.scan(add_lag, start, jnp.arange(NT, dtype=jnp.int32))
    return total.astype(jnp.bfloat16)
```

```python
import functools

import jax
import jax.numpy as jnp
from jax import lax
from jax.experimental import pallas as pl
from jax.experimental.pallas import tpu as pltpu
from jax.sharding import PartitionSpec as P

MESH = pl.DeviceIdType.MESH


def kernel(
    n, m, chunks, x_hbm, op_hbm, out_ref, x, op, acc, part, total, share,
    own_sem, op_sem, out_sem, pair_sem, fwd_sem, in_sem,
    red_out, red_in, floor_out, floor_in,
):
    me, floor = lax.axis_index("tm"), lax.axis_index("floor")
    chips = n // 2
    chip, core = lax.div(me, 2), lax.rem(me, 2)
    pair = 2 * chip + 1 - core
    k, width = x.shape[2], x.shape[3]
    sensors = op.shape[1]
    share_size = sensors // m

    def columns(c):
        return pl.ds(c * width, width)

    own = [pltpu.make_async_copy(x_hbm.at[0, :, columns(c)], x.at[c, me], own_sem.at[c]) for c in range(chunks)]
    weights = [pltpu.make_async_copy(op_hbm.at[0, :, columns(c)], op.at[c], op_sem.at[c]) for c in range(chunks)]
    for c in range(chunks):
        own[c].start()
        weights[c].start()

    barrier = pltpu.get_barrier_semaphore()
    for step in range(1, n):
        pl.semaphore_signal(barrier, inc=1, device_id={"tm": lax.rem(me + step, n)}, device_id_type=MESH)
    for step in range(1, m):
        pl.semaphore_signal(barrier, inc=1, device_id={"floor": lax.rem(floor + step, m)}, device_id_type=MESH)
    pl.semaphore_wait(barrier, n + m - 2)

    def need(block, at_chip):
        return 2 * at_chip + block < n

    def to_chip(c, step):
        other = lax.rem(chip + step, chips)
        copy = pltpu.make_async_remote_copy(
            src_ref=x_hbm.at[0, :, columns(c)], dst_ref=x.at[c, me],
            send_sem=out_sem.at[c, step], recv_sem=in_sem.at[c, me],
            device_id={"tm": 2 * other + core}, device_id_type=MESH,
        )
        return need(me, other), copy

    def to_pair(c):
        copy = pltpu.make_async_remote_copy(
            src_ref=x_hbm.at[0, :, columns(c)], dst_ref=x.at[c, me],
            send_sem=pair_sem.at[c], recv_sem=in_sem.at[c, me],
            device_id={"tm": pair}, device_id_type=MESH,
        )
        return need(me, chip), copy

    def forward(c, block):
        return pltpu.make_async_remote_copy(
            src_ref=x.at[c, block], dst_ref=x.at[c, block],
            send_sem=fwd_sem.at[c, block], recv_sem=in_sem.at[c, block],
            device_id={"tm": pair}, device_id_type=MESH,
        )

    def sends(act):
        for c in range(chunks):
            for step in range(chips - 1, 0, -1):
                wanted, copy = to_chip(c, step)
                pl.when(wanted)(functools.partial(act, copy))
            wanted, copy = to_pair(c)
            pl.when(wanted)(functools.partial(act, copy))

    sends(lambda copy: copy.start())

    def take_and_forward(c):
        for step in range(1, chips):
            block = 2 * lax.rem(chip + step, chips) + core

            @pl.when(need(block, chip))
            def _():
                copy = forward(c, block)
                copy.wait_recv()
                copy.start()

    def take(c):
        for step in range(chips):
            block = 2 * lax.rem(chip + step, chips) + 1 - core

            @pl.when(need(block, chip))
            def _():
                forward(c, block).wait_recv()

    tile = min(n, max(1, 128 // k))

    take_and_forward(0)
    for c in range(chunks):
        if c + 1 < chunks:
            take_and_forward(c + 1)
        take(c)
        own[c].wait()
        weights[c].wait()
        for r in range(n // tile):
            rows = x[c, r * tile:(r + 1) * tile].reshape(tile * k, width)
            image = lax.dot_general(
                rows, op[c], (((1,), (1,)), ((), ())), preferred_element_type=jnp.float32
            ).reshape(tile, k, sensors)
            if c == 0:
                acc[r * tile:(r + 1) * tile] = image
            else:
                acc[r * tile:(r + 1) * tile] += image

    def lag_part(step):
        return pltpu.make_async_remote_copy(
            src_ref=acc.at[step], dst_ref=part.at[me],
            send_sem=red_out.at[step], recv_sem=red_in.at[me],
            device_id={"tm": lax.rem(me + step, n)}, device_id_type=MESH,
        )

    for step in range(n - 1, 0, -1):
        @pl.when(me + step < n)
        def _(step=step):
            lag_part(step).start()

    def add_lag(lag, value):
        pltpu.make_async_remote_copy(
            src_ref=acc.at[0], dst_ref=part.at[lag],
            send_sem=red_out.at[0], recv_sem=red_in.at[lag],
            device_id={"tm": pair}, device_id_type=MESH,
        ).wait_recv()
        return value + part[lag]

    value = lax.fori_loop(0, me, add_lag, acc[0])
    for j in range(m):
        total[j] = value[:, j * share_size:(j + 1) * share_size]

    def to_floor(step):
        other = lax.rem(floor + step, m)
        return pltpu.make_async_remote_copy(
            src_ref=total.at[other], dst_ref=share.at[floor],
            send_sem=floor_out.at[step], recv_sem=floor_in.at[floor],
            device_id={"floor": other}, device_id_type=MESH,
        )

    for step in range(m - 1, 0, -1):
        to_floor(step).start()
    result = total[floor]
    for step in range(1, m):
        source = lax.rem(floor + step, m)
        pltpu.make_async_remote_copy(
            src_ref=total.at[source], dst_ref=share.at[source],
            send_sem=floor_out.at[step], recv_sem=floor_in.at[source],
            device_id={"floor": source}, device_id_type=MESH,
        ).wait_recv()
        result = result + share[source]
    out_ref[0] = result.astype(out_ref.dtype)

    sends(lambda copy: copy.wait_send())
    for c in range(chunks):
        for step in range(1, chips):
            block = 2 * lax.rem(chip + step, chips) + core

            @pl.when(need(block, chip))
            def _(c=c, block=block):
                forward(c, block).wait_send()
    for step in range(n - 1, 0, -1):
        @pl.when(me + step < n)
        def _(step=step):
            lag_part(step).wait_send()
    for step in range(1, m):
        to_floor(step).wait_send()


def solution(mesh):
    n, m = mesh.shape["tm"], mesh.shape["floor"]

    def local(samples, operator):
        _, k, depth = samples.shape
        sensors = operator.shape[1]
        chunks = 8
        width = depth // chunks
        return pl.pallas_call(
            functools.partial(kernel, n, m, chunks),
            out_shape=jax.ShapeDtypeStruct((1, k, sensors // m), jnp.bfloat16),
            in_specs=[pl.BlockSpec(memory_space=pl.ANY)] * 2,
            out_specs=pl.BlockSpec(memory_space=pltpu.VMEM),
            scratch_shapes=[
                pltpu.VMEM((chunks, n, k, width), jnp.bfloat16),
                pltpu.VMEM((chunks, sensors, width), jnp.bfloat16),
                pltpu.VMEM((n, k, sensors), jnp.float32),
                pltpu.VMEM((n, k, sensors), jnp.float32),
                pltpu.VMEM((m, k, sensors // m), jnp.float32),
                pltpu.VMEM((m, k, sensors // m), jnp.float32),
                pltpu.SemaphoreType.DMA((chunks,)),
                pltpu.SemaphoreType.DMA((chunks,)),
                pltpu.SemaphoreType.DMA((chunks, n // 2)),
                pltpu.SemaphoreType.DMA((chunks,)),
                pltpu.SemaphoreType.DMA((chunks, n)),
                pltpu.SemaphoreType.DMA((chunks, n)),
                pltpu.SemaphoreType.DMA((n,)),
                pltpu.SemaphoreType.DMA((n,)),
                pltpu.SemaphoreType.DMA((m,)),
                pltpu.SemaphoreType.DMA((m,)),
            ],
            compiler_params=pltpu.CompilerParams(collective_id=0, has_side_effects=True),
        )(samples, operator)

    placed = (P("tm", None, "floor"), P("tm", None, "floor"))
    return jax.shard_map(
        local, mesh=mesh, in_specs=placed, out_specs=P("tm", None, "floor"), check_vma=False
    )
```

```python
import functools

import jax
import jax.numpy as jnp
from jax import lax
from jax.experimental import pallas as pl
from jax.experimental.pallas import tpu as pltpu
from jax.sharding import PartitionSpec as P

MESH = pl.DeviceIdType.MESH
AHEAD, LOOK = 4, 4


def each(low, high, body):
    if high - low <= 4:
        for i in range(low, high):
            body(i)
    else:
        def step(i, carry):
            body(i)
            return carry

        lax.fori_loop(low, high, step, 0)


def grid_of(chips):
    rows = 1
    while rows * rows * 4 <= chips and chips % (rows * 2) == 0:
        rows *= 2
    return rows, chips // rows


def kernel(
    n, m, chunks, x_hbm, op_hbm, out_ref, x, op, acc, part, total, share,
    own_sem, op_sem, out_sem, pair_sem, fwd_sem, relay_sem, in_sem,
    red_out, red_in, floor_out, floor_in,
):
    me, floor = lax.axis_index("tm"), lax.axis_index("floor")
    chips = n // 2
    rows, cols = grid_of(chips)
    chip, core = lax.div(me, 2), lax.rem(me, 2)
    row, col = lax.div(chip, cols), lax.rem(chip, cols)
    pair = 2 * chip + 1 - core
    k, width = x.shape[2], x.shape[3]
    sensors = op.shape[1]
    share_size = sensors // m

    def columns(c):
        return pl.ds(c * width, width)

    own = [pltpu.make_async_copy(x_hbm.at[0, :, columns(c)], x.at[c, me], own_sem.at[c]) for c in range(chunks)]
    weights = [pltpu.make_async_copy(op_hbm.at[0, :, columns(c)], op.at[c], op_sem.at[c]) for c in range(chunks)]
    for c in range(chunks):
        own[c].start()
        weights[c].start()

    barrier = pltpu.get_barrier_semaphore()
    for step in range(1, n):
        pl.semaphore_signal(barrier, inc=1, device_id={"tm": lax.rem(me + step, n)}, device_id_type=MESH)
    for step in range(1, m):
        pl.semaphore_signal(barrier, inc=1, device_id={"floor": lax.rem(floor + step, m)}, device_id_type=MESH)
    pl.semaphore_wait(barrier, n + m - 2)

    def need(block, at_chip):
        return 2 * at_chip + block < n

    many = max(rows, cols)

    def relayed(odd, source, block, at, step):
        turn = lax.rem(core + odd, 2) == 0
        r, q = lax.div(source, cols), lax.rem(source, cols)
        r_at, q_at = lax.div(at, cols), lax.rem(at, cols)
        r_to, q_to = lax.rem(r + step, rows), lax.rem(q + step, cols)
        down = (r_at == r) & (step < rows) & (turn | ((r_to == 0) & (q == 0)))
        along = (q_at == q) & (step < cols) & (jnp.logical_not(turn) | ((q_to == 0) & (r == 0)))
        target = jnp.where(r_at == r, r_to * cols + q_at, r_at * cols + q_to)
        return (at != 0) & (down | along) & need(block, target), 2 * target + core

    def route(odd, source, block, at):
        passes = at < 0
        for step in range(1, many):
            passes = passes | relayed(odd, source, block, at, step)[0]
        straight = (lax.div(source, cols) == lax.div(at, cols)) | (lax.rem(source, cols) == lax.rem(at, cols))
        return straight & (need(block, at) | passes), passes

    def make_plan(step, odd):
        other = lax.rem(chip + step, chips)
        block = 2 * other + core
        wanted, _ = route(odd, chip, me, other)
        _, passes = route(odd, other, block, chip)
        here = need(block, chip)
        alone = here & jnp.logical_not(passes)
        onward = [relayed(odd, other, block, chip, s) for s in range(1, many)]
        return other, block, wanted, passes, here, alone, onward

    plans = {}
    if chips <= 5:
        plans = {(step, odd): make_plan(step, odd) for step in range(1, chips) for odd in (0, 1)}

    def plan(step, c):
        return plans[step, c % 2] if plans else make_plan(step, c % 2)

    others = [2 * lax.rem(chip + step, chips) + 1 - core for step in range(chips)] if plans else None
    others_here = [need(block, chip) for block in others] if plans else None
    self_here = need(me, chip)

    def send(c, block, target, sem, first=False):
        return pltpu.make_async_remote_copy(
            src_ref=x_hbm.at[0, :, columns(c)] if first else x.at[c, block], dst_ref=x.at[c, block],
            send_sem=sem, recv_sem=in_sem.at[c, block], device_id={"tm": target}, device_id_type=MESH,
        )

    def sends(c, act):
        def one(step):
            _, block, wanted, *_ = plan(step, c)

            @pl.when(wanted)
            def _():
                act(send(c, me, block, out_sem.at[c, step], True))

        each(1, chips, one)

        @pl.when(self_here)
        def _():
            act(send(c, me, pair, pair_sem.at[c], True))

    def relays(c, act, wait):
        def one(step):
            source, block, _, passes, _, _, onward = plan(step, c)

            @pl.when(passes)
            def _():
                if wait:
                    send(c, block, pair, fwd_sem.at[c, source]).wait_recv()
                for s, (wanted, target) in enumerate(onward):
                    @pl.when(wanted)
                    def _(s=s, target=target):
                        act(send(c, block, target, relay_sem.at[c, source, s]))

        each(1, chips, one)

    def forwards(c, act, wait):
        def one(step):
            source, block, _, _, here, alone, _ = plan(step, c)
            if wait:
                @pl.when(alone)
                def _():
                    send(c, block, pair, fwd_sem.at[c, source]).wait_recv()

            @pl.when(here)
            def _():
                act(send(c, block, pair, fwd_sem.at[c, source]))

        each(1, chips, one)

    def take(c):
        def one(step):
            block = others[step] if plans else 2 * lax.rem(chip + step, chips) + 1 - core
            here = others_here[step] if plans else need(block, chip)

            @pl.when(here)
            def _():
                send(c, block, pair, pair_sem.at[c]).wait_recv()

        each(0, chips, one)

    def start(copy):
        copy.start()

    def wait_send(copy):
        copy.wait_send()

    for c in range(min(AHEAD, chunks)):
        sends(c, start)

    tile = min(n, max(1, 128 // k))

    def pass_on(c):
        if c < chunks:
            relays(c, start, True)
        if c + AHEAD < chunks:
            sends(c + AHEAD, start)

    for c in range(min(LOOK, chunks)):
        pass_on(c)
    forwards(0, start, True)
    for c in range(chunks):
        pass_on(c + LOOK)
        if c + 1 < chunks:
            forwards(c + 1, start, True)
        take(c)
        own[c].wait()
        weights[c].wait()
        for r in range(n // tile):
            block_rows = x[c, r * tile:(r + 1) * tile].reshape(tile * k, width)
            image = lax.dot_general(
                block_rows, op[c], (((1,), (1,)), ((), ())), preferred_element_type=jnp.float32
            ).reshape(tile, k, sensors)
            if c == 0:
                acc[r * tile:(r + 1) * tile] = image
            else:
                acc[r * tile:(r + 1) * tile] += image

    def lag_part(step):
        return pltpu.make_async_remote_copy(
            src_ref=acc.at[step], dst_ref=part.at[me],
            send_sem=red_out.at[step], recv_sem=red_in.at[me],
            device_id={"tm": lax.rem(me + step, n)}, device_id_type=MESH,
        )

    for step in range(n - 1, 0, -1):
        @pl.when(me + step < n)
        def _(step=step):
            lag_part(step).start()

    for c in range(chunks):
        sends(c, wait_send)
        relays(c, wait_send, False)
        forwards(c, wait_send, False)

    def add_lag(lag, value):
        pltpu.make_async_remote_copy(
            src_ref=acc.at[0], dst_ref=part.at[lag],
            send_sem=red_out.at[0], recv_sem=red_in.at[lag],
            device_id={"tm": pair}, device_id_type=MESH,
        ).wait_recv()
        return value + part[lag]

    value = lax.fori_loop(0, me, add_lag, acc[0])
    for j in range(m):
        total[j] = value[:, j * share_size:(j + 1) * share_size]

    def to_floor(step):
        other = lax.rem(floor + step, m)
        return pltpu.make_async_remote_copy(
            src_ref=total.at[other], dst_ref=share.at[floor],
            send_sem=floor_out.at[step], recv_sem=floor_in.at[floor],
            device_id={"floor": other}, device_id_type=MESH,
        )

    for step in range(m - 1, 0, -1):
        to_floor(step).start()
    result = total[floor]
    for step in range(1, m):
        source = lax.rem(floor + step, m)
        pltpu.make_async_remote_copy(
            src_ref=total.at[source], dst_ref=share.at[source],
            send_sem=floor_out.at[step], recv_sem=floor_in.at[source],
            device_id={"floor": source}, device_id_type=MESH,
        ).wait_recv()
        result = result + share[source]
    out_ref[0] = result.astype(out_ref.dtype)

    for step in range(n - 1, 0, -1):
        @pl.when(me + step < n)
        def _(step=step):
            lag_part(step).wait_send()
    for step in range(1, m):
        to_floor(step).wait_send()


def solution(mesh):
    n, m = mesh.shape["tm"], mesh.shape["floor"]

    def local(samples, operator):
        _, k, depth = samples.shape
        sensors = operator.shape[1]
        chunks = 4
        width = depth // chunks
        return pl.pallas_call(
            functools.partial(kernel, n, m, chunks),
            out_shape=jax.ShapeDtypeStruct((1, k, sensors // m), jnp.bfloat16),
            in_specs=[pl.BlockSpec(memory_space=pl.ANY)] * 2,
            out_specs=pl.BlockSpec(memory_space=pltpu.VMEM),
            scratch_shapes=[
                pltpu.VMEM((chunks, n, k, width), jnp.bfloat16),
                pltpu.VMEM((chunks, sensors, width), jnp.bfloat16),
                pltpu.VMEM((n, k, sensors), jnp.float32),
                pltpu.VMEM((n, k, sensors), jnp.float32),
                pltpu.VMEM((m, k, sensors // m), jnp.float32),
                pltpu.VMEM((m, k, sensors // m), jnp.float32),
                pltpu.SemaphoreType.DMA((chunks,)),
                pltpu.SemaphoreType.DMA((chunks,)),
                pltpu.SemaphoreType.DMA((chunks, n // 2)),
                pltpu.SemaphoreType.DMA((chunks,)),
                pltpu.SemaphoreType.DMA((chunks, n // 2)),
                pltpu.SemaphoreType.DMA((chunks, n // 2, max(1, max(grid_of(n // 2)) - 1))),
                pltpu.SemaphoreType.DMA((chunks, n)),
                pltpu.SemaphoreType.DMA((n,)),
                pltpu.SemaphoreType.DMA((n,)),
                pltpu.SemaphoreType.DMA((m,)),
                pltpu.SemaphoreType.DMA((m,)),
            ],
            compiler_params=pltpu.CompilerParams(collective_id=0, has_side_effects=True),
        )(samples, operator)

    placed = (P("tm", None, "floor"), P("tm", None, "floor"))
    return jax.shard_map(
        local, mesh=mesh, in_specs=placed, out_specs=P("tm", None, "floor"), check_vma=False
    )
```

```python
import functools

import jax
import jax.numpy as jnp
from jax import lax
from jax.experimental import pallas as pl
from jax.experimental.pallas import tpu as pltpu
from jax.sharding import PartitionSpec as P

MESH = pl.DeviceIdType.MESH
LOOK = 1


def each(low, high, body):
    if high - low <= 4:
        for i in range(low, high):
            body(i)
    else:
        def step(i, carry):
            body(i)
            return carry

        lax.fori_loop(low, high, step, 0)


def grid_of(chips):
    rows = 1
    while rows * rows * 4 <= chips and chips % (rows * 2) == 0:
        rows *= 2
    return rows, chips // rows


def kernel(
    n, m, chunks, x_hbm, op_hbm, out_ref, x, far, op, acc, part, total, share,
    own_sem, op_sem, out_sem, pair_sem, fwd_sem, relay_sem, in_sem,
    red_out, red_in, floor_out, floor_in,
):
    me, floor = lax.axis_index("tm"), lax.axis_index("floor")
    chips = n // 2
    rows, cols = grid_of(chips)
    chip, core = lax.div(me, 2), lax.rem(me, 2)
    row, col = lax.div(chip, cols), lax.rem(chip, cols)
    pair = 2 * chip + 1 - core
    k, width = x.shape[2], x.shape[3]
    sensors = op.shape[1]
    share_size = sensors // m

    def columns(c):
        return pl.ds(c * width, width)

    own = [pltpu.make_async_copy(x_hbm.at[0, :, columns(c)], x.at[c, me], own_sem.at[c]) for c in range(chunks)]
    weights = [pltpu.make_async_copy(op_hbm.at[0, :, columns(c)], op.at[c], op_sem.at[c]) for c in range(chunks)]
    for c in range(chunks):
        own[c].start()
        weights[c].start()

    barrier = pltpu.get_barrier_semaphore()
    for step in range(1, n):
        pl.semaphore_signal(barrier, inc=1, device_id={"tm": lax.rem(me + step, n)}, device_id_type=MESH)
    for step in range(1, m):
        pl.semaphore_signal(barrier, inc=1, device_id={"floor": lax.rem(floor + step, m)}, device_id_type=MESH)
    pl.semaphore_wait(barrier, n + m - 2)

    def need(block, at_chip):
        return 2 * at_chip + block < n

    many = max(rows, cols)

    def straight(source, at):
        return (lax.div(source, cols) == lax.div(at, cols)) | (lax.rem(source, cols) == lax.rem(at, cols))

    def relayed(odd, source, block, at, step):
        turn = lax.rem(core + odd, 2) == 0
        r, q = lax.div(source, cols), lax.rem(source, cols)
        r_at, q_at = lax.div(at, cols), lax.rem(at, cols)
        r_to, q_to = lax.rem(r + step, rows), lax.rem(q + step, cols)
        down = (r_at == r) & (step < rows) & (turn | ((r_to == 0) & (q == 0)))
        along = (q_at == q) & (step < cols) & (jnp.logical_not(turn) | ((q_to == 0) & (r == 0)))
        target = jnp.where(r_at == r, r_to * cols + q_at, r_at * cols + q_to)
        return (at != 0) & (down | along) & need(block, target), 2 * target + core

    def route(odd, source, block, at):
        passes = at < 0
        for step in range(1, many):
            passes = passes | relayed(odd, source, block, at, step)[0]
        return straight(source, at) & (need(block, at) | passes), passes

    def make_plan(step, odd):
        other = lax.rem(chip + step, chips)
        block = 2 * other + core
        wanted, _ = route(odd, chip, me, other)
        _, passes = route(odd, other, block, chip)
        near = straight(other, chip)
        here = need(block, chip) & near, need(block, chip) & jnp.logical_not(near)
        alone = here[0] & jnp.logical_not(passes)
        onward = [relayed(odd, other, block, chip, s) for s in range(1, many)]
        return other, block, wanted, passes, here, alone, onward

    plans = {}
    if chips <= 5:
        plans = {(step, odd): make_plan(step, odd) for step in range(1, chips) for odd in (0, 1)}

    def plan(step, c):
        return plans[step, c % 2] if plans else make_plan(step, c % 2)

    others = [2 * lax.rem(chip + step, chips) + 1 - core for step in range(chips)] if plans else None
    def other_here(block):
        near = straight(lax.div(block, 2), chip)
        return need(block, chip) & near, need(block, chip) & jnp.logical_not(near)

    others_here = [other_here(block) for block in others] if plans else None
    self_here = need(me, chip)

    busy = need(2 * row * cols, chip) | need(2 * col, chip)

    def send(c, block, target, sem, source=None, into=None):
        return pltpu.make_async_remote_copy(
            src_ref=x.at[c, block] if source is None else source,
            dst_ref=(x if into is None else into).at[c, block],
            send_sem=sem, recv_sem=in_sem.at[c, block], device_id={"tm": target}, device_id_type=MESH,
        )

    def mine(c):
        return x_hbm.at[0, :, columns(c)]

    def sends(c, act):
        def one(step):
            _, block, wanted, *_ = plan(step, c)

            @pl.when(wanted)
            def _():
                act(send(c, me, block, out_sem.at[c, step], mine(c)))

        each(1, chips, one)

        @pl.when(self_here)
        def _():
            act(send(c, me, pair, pair_sem.at[c], mine(c)))

    def relays(c, act, wait):
        def one(step):
            source, block, _, passes, _, _, onward = plan(step, c)

            @pl.when(passes)
            def _():
                if wait:
                    send(c, block, pair, fwd_sem.at[c, source]).wait_recv()
                for s, (wanted, target) in enumerate(onward):
                    @pl.when(wanted)
                    def _(s=s, target=target):
                        act(send(c, block, target, relay_sem.at[c, source, s], None, far))

        each(1, chips, one)

    def forwards(c, act, wait):
        def one(step):
            source, block, _, _, here, alone, _ = plan(step, c)
            if wait:
                @pl.when(alone)
                def _():
                    send(c, block, pair, fwd_sem.at[c, source]).wait_recv()

            @pl.when(here[0])
            def _():
                act(send(c, block, pair, fwd_sem.at[c, source]))

        each(1, chips, one)

    def far_forwards(c, act, wait):
        def one(step):
            source, block, _, _, here, _, _ = plan(step, c)

            @pl.when(here[1])
            def _():
                copy = send(c, block, pair, fwd_sem.at[c, source], far.at[c, block], far)
                if wait:
                    copy.wait_recv()
                act(copy)

        each(1, chips, one)

    def take(c, part_of):
        def one(step):
            block = others[step] if plans else 2 * lax.rem(chip + step, chips) + 1 - core
            here = (others_here[step] if plans else other_here(block))[part_of]

            @pl.when(here)
            def _():
                send(c, block, pair, pair_sem.at[c], None, far if part_of else None).wait_recv()

        each(0, chips, one)

    def start(copy):
        copy.start()

    def wait_send(copy):
        copy.wait_send()


    tile = min(n, max(1, 128 // k))

    def image_of(block_rows, c):
        return lax.dot_general(
            block_rows.reshape(-1, width), op[c], (((1,), (1,)), ((), ())), preferred_element_type=jnp.float32
        ).reshape(-1, k, sensors)

    for c in range(chunks):
        sends(c, start)
    for c in range(min(LOOK, chunks)):
        relays(c, start, True)
    forwards(0, start, True)
    for c in range(chunks):
        if c + LOOK < chunks:
            relays(c + LOOK, start, True)
        if c + 1 < chunks:
            forwards(c + 1, start, True)
        take(c, 0)
        own[c].wait()
        weights[c].wait()

        @pl.when(busy)
        def _(c=c):
            for r in range(n // tile):
                image = image_of(x[c, r * tile:(r + 1) * tile], c)
                if c == 0:
                    acc[r * tile:(r + 1) * tile] = image
                else:
                    acc[r * tile:(r + 1) * tile] += image

    def lag_part(step):
        return pltpu.make_async_remote_copy(
            src_ref=acc.at[step], dst_ref=part.at[me],
            send_sem=red_out.at[step], recv_sem=red_in.at[me],
            device_id={"tm": lax.rem(me + step, n)}, device_id_type=MESH,
        )

    def lag_parts(near, act):
        for step in range(n - 1, 0, -1):
            @pl.when((me + step < n) & (straight(step // 2, chip) == near))
            def _(step=step):
                act(lag_part(step))

    lag_parts(True, start)

    far_forwards(0, start, True)
    for c in range(chunks):
        if c + 1 < chunks:
            far_forwards(c + 1, start, True)
        take(c, 1)

        def far_images(step, c=c):
            r = lax.rem(row + 1 + lax.div(step, max(1, cols - 1)), rows)
            q = lax.rem(col + 1 + lax.rem(step, max(1, cols - 1)), cols)
            source = r * cols + q

            @pl.when(need(2 * source, chip))
            def _():
                image = image_of(far[c, pl.ds(2 * source, 2)], c)
                if c == 0:
                    acc[pl.ds(2 * source, 2)] = image
                else:
                    acc[pl.ds(2 * source, 2)] += image

        each(0, (rows - 1) * (cols - 1), far_images)

    lag_parts(False, start)

    for c in range(chunks):
        sends(c, wait_send)
        relays(c, wait_send, False)
        forwards(c, wait_send, False)
        far_forwards(c, wait_send, False)

    def add_lag(lag, value):
        pltpu.make_async_remote_copy(
            src_ref=acc.at[0], dst_ref=part.at[lag],
            send_sem=red_out.at[0], recv_sem=red_in.at[lag],
            device_id={"tm": pair}, device_id_type=MESH,
        ).wait_recv()
        return value + part[lag]

    value = lax.fori_loop(0, me, add_lag, acc[0])
    for j in range(m):
        total[j] = value[:, j * share_size:(j + 1) * share_size]

    def to_floor(step):
        other = lax.rem(floor + step, m)
        return pltpu.make_async_remote_copy(
            src_ref=total.at[other], dst_ref=share.at[floor],
            send_sem=floor_out.at[step], recv_sem=floor_in.at[floor],
            device_id={"floor": other}, device_id_type=MESH,
        )

    for step in range(m - 1, 0, -1):
        to_floor(step).start()
    result = total[floor]
    for step in range(1, m):
        source = lax.rem(floor + step, m)
        pltpu.make_async_remote_copy(
            src_ref=total.at[source], dst_ref=share.at[source],
            send_sem=floor_out.at[step], recv_sem=floor_in.at[source],
            device_id={"floor": source}, device_id_type=MESH,
        ).wait_recv()
        result = result + share[source]
    out_ref[0] = result.astype(out_ref.dtype)

    lag_parts(True, wait_send)
    lag_parts(False, wait_send)
    for step in range(1, m):
        to_floor(step).wait_send()


def solution(mesh):
    n, m = mesh.shape["tm"], mesh.shape["floor"]

    def local(samples, operator):
        _, k, depth = samples.shape
        sensors = operator.shape[1]
        chunks = 4
        width = depth // chunks
        return pl.pallas_call(
            functools.partial(kernel, n, m, chunks),
            out_shape=jax.ShapeDtypeStruct((1, k, sensors // m), jnp.bfloat16),
            in_specs=[pl.BlockSpec(memory_space=pl.ANY)] * 2,
            out_specs=pl.BlockSpec(memory_space=pltpu.VMEM),
            scratch_shapes=[
                pltpu.VMEM((chunks, n, k, width), jnp.bfloat16),
                pltpu.VMEM((chunks, n, k, width), jnp.bfloat16),
                pltpu.VMEM((chunks, sensors, width), jnp.bfloat16),
                pltpu.VMEM((n, k, sensors), jnp.float32),
                pltpu.VMEM((n, k, sensors), jnp.float32),
                pltpu.VMEM((m, k, sensors // m), jnp.float32),
                pltpu.VMEM((m, k, sensors // m), jnp.float32),
                pltpu.SemaphoreType.DMA((chunks,)),
                pltpu.SemaphoreType.DMA((chunks,)),
                pltpu.SemaphoreType.DMA((chunks, n // 2)),
                pltpu.SemaphoreType.DMA((chunks,)),
                pltpu.SemaphoreType.DMA((chunks, n // 2)),
                pltpu.SemaphoreType.DMA((chunks, n // 2, max(1, max(grid_of(n // 2)) - 1))),
                pltpu.SemaphoreType.DMA((chunks, n)),
                pltpu.SemaphoreType.DMA((n,)),
                pltpu.SemaphoreType.DMA((n,)),
                pltpu.SemaphoreType.DMA((m,)),
                pltpu.SemaphoreType.DMA((m,)),
            ],
            compiler_params=pltpu.CompilerParams(collective_id=0, has_side_effects=True),
        )(samples, operator)

    placed = (P("tm", None, "floor"), P("tm", None, "floor"))
    return jax.shard_map(
        local, mesh=mesh, in_specs=placed, out_specs=P("tm", None, "floor"), check_vma=False
    )
```

```python
import functools

import jax
import jax.numpy as jnp
from jax import lax
from jax.experimental import pallas as pl
from jax.experimental.pallas import tpu as pltpu
from jax.sharding import PartitionSpec as P

MESH = pl.DeviceIdType.MESH
LOOK = 1


def each(low, high, body):
    if high - low <= 4:
        for i in range(low, high):
            body(i)
    else:
        def step(i, carry):
            body(i)
            return carry

        lax.fori_loop(low, high, step, 0)


def grid_of(chips):
    rows = 1
    while rows * rows * 4 <= chips and chips % (rows * 2) == 0:
        rows *= 2
    return rows, chips // rows


def kernel(
    n, m, chunks, x_hbm, op_hbm, out_ref, x, far, op, acc, part, total, share,
    own_sem, op_sem, out_sem, pair_sem, fwd_sem, relay_sem, in_sem,
    red_out, red_in, floor_out, floor_in, up_sem, down_sem,
):
    me, floor = lax.axis_index("tm"), lax.axis_index("floor")
    chips = n // 2
    rows, cols = grid_of(chips)
    chip, core = lax.div(me, 2), lax.rem(me, 2)
    row, col = lax.div(chip, cols), lax.rem(chip, cols)
    pair = 2 * chip + 1 - core
    k, width = x.shape[2], x.shape[3]
    sensors = op.shape[1]
    share_size = sensors // m

    def columns(c):
        return pl.ds(c * width, width)

    own = [pltpu.make_async_copy(x_hbm.at[0, :, columns(c)], x.at[c, me], own_sem.at[c]) for c in range(chunks)]
    weights = [pltpu.make_async_copy(op_hbm.at[0, :, columns(c)], op.at[c], op_sem.at[c]) for c in range(chunks)]
    for c in range(chunks):
        own[c].start()
        weights[c].start()

    barrier = pltpu.get_barrier_semaphore()
    for step in range(1, n):
        pl.semaphore_signal(barrier, inc=1, device_id={"tm": lax.rem(me + step, n)}, device_id_type=MESH)
    below, above = floor > 0, floor < m - 1

    @pl.when(below)
    def _():
        pl.semaphore_signal(barrier, inc=1, device_id={"floor": floor - 1}, device_id_type=MESH)

    @pl.when(above)
    def _():
        pl.semaphore_signal(barrier, inc=1, device_id={"floor": floor + 1}, device_id_type=MESH)

    pl.semaphore_wait(barrier, n - 1 + jnp.where(below, 1, 0) + jnp.where(above, 1, 0))

    def words(turn):
        for sem, place, target in ((up_sem, floor, floor + 1), (down_sem, m - 1 - floor, floor - 1)):
            @pl.when(place == turn)
            def _(sem=sem, target=target):
                if turn > 0:
                    pl.semaphore_wait(sem, 1)
                if turn < m - 1:
                    pl.semaphore_signal(sem, inc=1, device_id={"floor": target}, device_id_type=MESH)

    def need(block, at_chip):
        return 2 * at_chip + block < n

    many = max(rows, cols)

    def straight(source, at):
        return (lax.div(source, cols) == lax.div(at, cols)) | (lax.rem(source, cols) == lax.rem(at, cols))

    def relayed(odd, source, block, at, step):
        turn = lax.rem(core + odd, 2) == 0
        r, q = lax.div(source, cols), lax.rem(source, cols)
        r_at, q_at = lax.div(at, cols), lax.rem(at, cols)
        r_to, q_to = lax.rem(r + step, rows), lax.rem(q + step, cols)
        down = (r_at == r) & (step < rows) & (turn | ((r_to == 0) & (q == 0)))
        along = (q_at == q) & (step < cols) & (jnp.logical_not(turn) | ((q_to == 0) & (r == 0)))
        target = jnp.where(r_at == r, r_to * cols + q_at, r_at * cols + q_to)
        return (at != 0) & (down | along) & need(block, target), 2 * target + core

    def route(odd, source, block, at):
        passes = at < 0
        for step in range(1, many):
            passes = passes | relayed(odd, source, block, at, step)[0]
        return straight(source, at) & (need(block, at) | passes), passes

    def make_plan(step, odd):
        other = lax.rem(chip + step, chips)
        block = 2 * other + core
        wanted, _ = route(odd, chip, me, other)
        _, passes = route(odd, other, block, chip)
        near = straight(other, chip)
        here = need(block, chip) & near, need(block, chip) & jnp.logical_not(near)
        alone = here[0] & jnp.logical_not(passes)
        onward = [relayed(odd, other, block, chip, s) for s in range(1, many)]
        return other, block, wanted, passes, here, alone, onward

    plans = {}
    if chips <= 5:
        plans = {(step, odd): make_plan(step, odd) for step in range(1, chips) for odd in (0, 1)}

    def plan(step, c):
        return plans[step, c % 2] if plans else make_plan(step, c % 2)

    others = [2 * lax.rem(chip + step, chips) + 1 - core for step in range(chips)] if plans else None
    def other_here(block):
        near = straight(lax.div(block, 2), chip)
        return need(block, chip) & near, need(block, chip) & jnp.logical_not(near)

    others_here = [other_here(block) for block in others] if plans else None
    self_here = need(me, chip)

    busy = need(2 * row * cols, chip) | need(2 * col, chip)

    def send(c, block, target, sem, source=None, into=None):
        return pltpu.make_async_remote_copy(
            src_ref=x.at[c, block] if source is None else source,
            dst_ref=(x if into is None else into).at[c, block],
            send_sem=sem, recv_sem=in_sem.at[c, block], device_id={"tm": target}, device_id_type=MESH,
        )

    def mine(c):
        return x_hbm.at[0, :, columns(c)]

    def sends(c, act):
        def one(step):
            _, block, wanted, *_ = plan(step, c)

            @pl.when(wanted)
            def _():
                act(send(c, me, block, out_sem.at[c, step], mine(c)))

        each(1, chips, one)

        @pl.when(self_here)
        def _():
            act(send(c, me, pair, pair_sem.at[c], mine(c)))

    def relays(c, act, wait):
        def one(step):
            source, block, _, passes, _, _, onward = plan(step, c)

            @pl.when(passes)
            def _():
                if wait:
                    send(c, block, pair, fwd_sem.at[c, source]).wait_recv()
                for s, (wanted, target) in enumerate(onward):
                    @pl.when(wanted)
                    def _(s=s, target=target):
                        act(send(c, block, target, relay_sem.at[c, source, s], None, far))

        each(1, chips, one)

    def forwards(c, act, wait):
        def one(step):
            source, block, _, _, here, alone, _ = plan(step, c)
            if wait:
                @pl.when(alone)
                def _():
                    send(c, block, pair, fwd_sem.at[c, source]).wait_recv()

            @pl.when(here[0])
            def _():
                act(send(c, block, pair, fwd_sem.at[c, source]))

        each(1, chips, one)

    def far_forwards(c, act, wait):
        def one(step):
            source, block, _, _, here, _, _ = plan(step, c)

            @pl.when(here[1])
            def _():
                copy = send(c, block, pair, fwd_sem.at[c, source], far.at[c, block], far)
                if wait:
                    copy.wait_recv()
                act(copy)

        each(1, chips, one)

    def take(c, part_of):
        def one(step):
            block = others[step] if plans else 2 * lax.rem(chip + step, chips) + 1 - core
            here = (others_here[step] if plans else other_here(block))[part_of]

            @pl.when(here)
            def _():
                send(c, block, pair, pair_sem.at[c], None, far if part_of else None).wait_recv()

        each(0, chips, one)

    def start(copy):
        copy.start()

    def wait_send(copy):
        copy.wait_send()


    tile = min(n, max(1, 128 // k))

    def image_of(block_rows, c):
        return lax.dot_general(
            block_rows.reshape(-1, width), op[c], (((1,), (1,)), ((), ())), preferred_element_type=jnp.float32
        ).reshape(-1, k, sensors)

    for c in range(chunks):
        sends(c, start)
    for c in range(min(LOOK, chunks)):
        relays(c, start, True)
    forwards(0, start, True)
    for c in range(chunks):
        if c + LOOK < chunks:
            relays(c + LOOK, start, True)
        if c + 1 < chunks:
            forwards(c + 1, start, True)
        take(c, 0)
        if c < m:
            words(c)
        own[c].wait()
        weights[c].wait()

        @pl.when(busy)
        def _(c=c):
            for r in range(n // tile):
                image = image_of(x[c, r * tile:(r + 1) * tile], c)
                if c == 0:
                    acc[r * tile:(r + 1) * tile] = image
                else:
                    acc[r * tile:(r + 1) * tile] += image

    def lag_part(step):
        return pltpu.make_async_remote_copy(
            src_ref=acc.at[step], dst_ref=part.at[me],
            send_sem=red_out.at[step], recv_sem=red_in.at[me],
            device_id={"tm": lax.rem(me + step, n)}, device_id_type=MESH,
        )

    def lag_parts(near, act):
        for step in range(n - 1, 0, -1):
            @pl.when((me + step < n) & (straight(step // 2, chip) == near))
            def _(step=step):
                act(lag_part(step))

    lag_parts(True, start)
    for turn in range(chunks, m):
        words(turn)

    far_forwards(0, start, True)
    for c in range(chunks):
        if c + 1 < chunks:
            far_forwards(c + 1, start, True)
        take(c, 1)

        def far_images(step, c=c):
            r = lax.rem(row + 1 + lax.div(step, max(1, cols - 1)), rows)
            q = lax.rem(col + 1 + lax.rem(step, max(1, cols - 1)), cols)
            source = r * cols + q

            @pl.when(need(2 * source, chip))
            def _():
                image = image_of(far[c, pl.ds(2 * source, 2)], c)
                if c == 0:
                    acc[pl.ds(2 * source, 2)] = image
                else:
                    acc[pl.ds(2 * source, 2)] += image

        each(0, (rows - 1) * (cols - 1), far_images)

    lag_parts(False, start)

    for c in range(chunks):
        sends(c, wait_send)
        relays(c, wait_send, False)
        forwards(c, wait_send, False)
        far_forwards(c, wait_send, False)

    def add_lag(lag, value):
        pltpu.make_async_remote_copy(
            src_ref=acc.at[0], dst_ref=part.at[lag],
            send_sem=red_out.at[0], recv_sem=red_in.at[lag],
            device_id={"tm": pair}, device_id_type=MESH,
        ).wait_recv()
        return value + part[lag]

    value = lax.fori_loop(0, me, add_lag, acc[0])
    for j in range(m):
        total[j] = value[:, j * share_size:(j + 1) * share_size]

    def to_floor(step):
        other = lax.rem(floor + step, m)
        return pltpu.make_async_remote_copy(
            src_ref=total.at[other], dst_ref=share.at[floor],
            send_sem=floor_out.at[step], recv_sem=floor_in.at[floor],
            device_id={"floor": other}, device_id_type=MESH,
        )

    for step in range(m - 1, 0, -1):
        to_floor(step).start()
    result = total[floor]
    for step in range(1, m):
        source = lax.rem(floor + step, m)
        pltpu.make_async_remote_copy(
            src_ref=total.at[source], dst_ref=share.at[source],
            send_sem=floor_out.at[step], recv_sem=floor_in.at[source],
            device_id={"floor": source}, device_id_type=MESH,
        ).wait_recv()
        result = result + share[source]
    out_ref[0] = result.astype(out_ref.dtype)

    lag_parts(True, wait_send)
    lag_parts(False, wait_send)
    for step in range(1, m):
        to_floor(step).wait_send()


def solution(mesh):
    n, m = mesh.shape["tm"], mesh.shape["floor"]

    def local(samples, operator):
        _, k, depth = samples.shape
        sensors = operator.shape[1]
        chunks = 4
        width = depth // chunks
        return pl.pallas_call(
            functools.partial(kernel, n, m, chunks),
            out_shape=jax.ShapeDtypeStruct((1, k, sensors // m), jnp.bfloat16),
            in_specs=[pl.BlockSpec(memory_space=pl.ANY)] * 2,
            out_specs=pl.BlockSpec(memory_space=pltpu.VMEM),
            scratch_shapes=[
                pltpu.VMEM((chunks, n, k, width), jnp.bfloat16),
                pltpu.VMEM((chunks, n, k, width), jnp.bfloat16),
                pltpu.VMEM((chunks, sensors, width), jnp.bfloat16),
                pltpu.VMEM((n, k, sensors), jnp.float32),
                pltpu.VMEM((n, k, sensors), jnp.float32),
                pltpu.VMEM((m, k, sensors // m), jnp.float32),
                pltpu.VMEM((m, k, sensors // m), jnp.float32),
                pltpu.SemaphoreType.DMA((chunks,)),
                pltpu.SemaphoreType.DMA((chunks,)),
                pltpu.SemaphoreType.DMA((chunks, n // 2)),
                pltpu.SemaphoreType.DMA((chunks,)),
                pltpu.SemaphoreType.DMA((chunks, n // 2)),
                pltpu.SemaphoreType.DMA((chunks, n // 2, max(1, max(grid_of(n // 2)) - 1))),
                pltpu.SemaphoreType.DMA((chunks, n)),
                pltpu.SemaphoreType.DMA((n,)),
                pltpu.SemaphoreType.DMA((n,)),
                pltpu.SemaphoreType.DMA((m,)),
                pltpu.SemaphoreType.DMA((m,)),
                pltpu.SemaphoreType.REGULAR,
                pltpu.SemaphoreType.REGULAR,
            ],
            compiler_params=pltpu.CompilerParams(collective_id=0, has_side_effects=True),
        )(samples, operator)

    placed = (P("tm", None, "floor"), P("tm", None, "floor"))
    return jax.shard_map(
        local, mesh=mesh, in_specs=placed, out_specs=P("tm", None, "floor"), check_vma=False
    )
```

```python
import functools

import jax
import jax.numpy as jnp
from jax import lax
from jax.experimental import pallas as pl
from jax.experimental.pallas import tpu as pltpu
from jax.sharding import PartitionSpec as P

MESH = pl.DeviceIdType.MESH
LOOK = 1


def each(low, high, body):
    if high - low <= 4:
        for i in range(low, high):
            body(i)
    else:
        def step(i, carry):
            body(i)
            return carry

        lax.fori_loop(low, high, step, 0)


def grid_of(chips):
    rows = 1
    while rows * rows * 4 <= chips and chips % (rows * 2) == 0:
        rows *= 2
    return rows, chips // rows


def kernel(
    n, m, chunks, x_hbm, op_hbm, out_ref, x, far, op, acc, part, total, share,
    own_sem, op_sem, out_sem, pair_sem, fwd_sem, relay_sem, in_sem,
    red_out, red_in, floor_out, floor_in, up_sem, down_sem,
):
    me, floor = lax.axis_index("tm"), lax.axis_index("floor")
    chips = n // 2
    rows, cols = grid_of(chips)
    chip, core = lax.div(me, 2), lax.rem(me, 2)
    row, col = lax.div(chip, cols), lax.rem(chip, cols)
    pair = 2 * chip + 1 - core
    k, width = x.shape[2], x.shape[3]
    sensors = op.shape[1]
    share_size = sensors // m

    def columns(c):
        return pl.ds(c * width, width)

    own = [pltpu.make_async_copy(x_hbm.at[0, :, columns(c)], x.at[c, me], own_sem.at[c]) for c in range(chunks)]
    weights = [pltpu.make_async_copy(op_hbm.at[0, :, columns(c)], op.at[c], op_sem.at[c]) for c in range(chunks)]
    for c in range(chunks):
        own[c].start()
        weights[c].start()

    barrier = pltpu.get_barrier_semaphore()
    for step in range(1, n):
        pl.semaphore_signal(barrier, inc=1, device_id={"tm": lax.rem(me + step, n)}, device_id_type=MESH)
    below, above = floor > 0, floor < m - 1

    @pl.when(below)
    def _():
        pl.semaphore_signal(barrier, inc=1, device_id={"floor": floor - 1}, device_id_type=MESH)

    @pl.when(above)
    def _():
        pl.semaphore_signal(barrier, inc=1, device_id={"floor": floor + 1}, device_id_type=MESH)

    pl.semaphore_wait(barrier, n - 1 + jnp.where(below, 1, 0) + jnp.where(above, 1, 0))

    def words(turn):
        for sem, place, target in ((up_sem, floor, floor + 1), (down_sem, m - 1 - floor, floor - 1)):
            @pl.when(place == turn)
            def _(sem=sem, target=target):
                if turn > 0:
                    pl.semaphore_wait(sem, 1)
                if turn < m - 1:
                    pl.semaphore_signal(sem, inc=1, device_id={"floor": target}, device_id_type=MESH)

    def need(block, at_chip):
        return 2 * at_chip + block < n

    many = max(rows, cols)

    def straight(source, at):
        return (lax.div(source, cols) == lax.div(at, cols)) | (lax.rem(source, cols) == lax.rem(at, cols))

    def relayed(odd, source, block, at, step):
        turn = lax.rem(core + odd, 2) == 0
        r, q = lax.div(source, cols), lax.rem(source, cols)
        r_at, q_at = lax.div(at, cols), lax.rem(at, cols)
        r_to, q_to = lax.rem(r + step, rows), lax.rem(q + step, cols)
        down = (r_at == r) & (step < rows) & (turn | ((r_to == 0) & (q == 0)))
        along = (q_at == q) & (step < cols) & (jnp.logical_not(turn) | ((q_to == 0) & (r == 0)))
        target = jnp.where(r_at == r, r_to * cols + q_at, r_at * cols + q_to)
        return (at != 0) & (down | along) & need(block, target), 2 * target + core

    def route(odd, source, block, at):
        passes = at < 0
        for step in range(1, many):
            passes = passes | relayed(odd, source, block, at, step)[0]
        return straight(source, at) & (need(block, at) | passes), passes

    def make_plan(step, odd):
        other = lax.rem(chip + step, chips)
        block = 2 * other + core
        wanted, _ = route(odd, chip, me, other)
        _, passes = route(odd, other, block, chip)
        near = straight(other, chip)
        here = need(block, chip) & near, need(block, chip) & jnp.logical_not(near)
        alone = here[0] & jnp.logical_not(passes)
        onward = [relayed(odd, other, block, chip, s) for s in range(1, many)]
        return other, block, wanted, passes, here, alone, onward

    plans = {}
    if chips <= 5:
        plans = {(step, odd): make_plan(step, odd) for step in range(1, chips) for odd in (0, 1)}

    def plan(step, c):
        return plans[step, c % 2] if plans else make_plan(step, c % 2)

    others = [2 * lax.rem(chip + step, chips) + 1 - core for step in range(chips)] if plans else None
    def other_here(block):
        near = straight(lax.div(block, 2), chip)
        return need(block, chip) & near, need(block, chip) & jnp.logical_not(near)

    others_here = [other_here(block) for block in others] if plans else None
    self_here = need(me, chip)

    busy = need(2 * row * cols, chip) | need(2 * col, chip)

    def send(c, block, target, sem, source=None, into=None):
        return pltpu.make_async_remote_copy(
            src_ref=x.at[c, block] if source is None else source,
            dst_ref=(x if into is None else into).at[c, block],
            send_sem=sem, recv_sem=in_sem.at[c, block], device_id={"tm": target}, device_id_type=MESH,
        )

    def mine(c):
        return x_hbm.at[0, :, columns(c)]

    def sends(c, act):
        def one(step):
            _, block, wanted, *_ = plan(step, c)

            @pl.when(wanted)
            def _():
                act(send(c, me, block, out_sem.at[c, step], mine(c)))

        each(1, chips, one)

        @pl.when(self_here)
        def _():
            act(send(c, me, pair, pair_sem.at[c], mine(c)))

    def relays(c, act, wait):
        def one(step):
            source, block, _, passes, _, _, onward = plan(step, c)

            @pl.when(passes)
            def _():
                if wait:
                    send(c, block, pair, fwd_sem.at[c, source]).wait_recv()
                for s, (wanted, target) in enumerate(onward):
                    @pl.when(wanted)
                    def _(s=s, target=target):
                        act(send(c, block, target, relay_sem.at[c, source, s], None, far))

        each(1, chips, one)

    def forwards(c, act, wait):
        def one(step):
            source, block, _, _, here, alone, _ = plan(step, c)
            if wait:
                @pl.when(alone)
                def _():
                    send(c, block, pair, fwd_sem.at[c, source]).wait_recv()

            @pl.when(here[0])
            def _():
                act(send(c, block, pair, fwd_sem.at[c, source]))

        each(1, chips, one)

    def far_forwards(c, act, wait):
        def one(step):
            source, block, _, _, here, _, _ = plan(step, c)

            @pl.when(here[1])
            def _():
                copy = send(c, block, pair, fwd_sem.at[c, source], far.at[c, block], far)
                if wait:
                    copy.wait_recv()
                act(copy)

        each(1, chips, one)

    def take(c, part_of):
        def one(step):
            block = others[step] if plans else 2 * lax.rem(chip + step, chips) + 1 - core
            here = (others_here[step] if plans else other_here(block))[part_of]

            @pl.when(here)
            def _():
                send(c, block, pair, pair_sem.at[c], None, far if part_of else None).wait_recv()

        each(0, chips, one)

    def start(copy):
        copy.start()

    def wait_send(copy):
        copy.wait_send()


    tile = min(n, max(1, 128 // k))

    def image_of(block_rows, c):
        return lax.dot_general(
            block_rows.reshape(-1, width), op[c], (((1,), (1,)), ((), ())), preferred_element_type=jnp.float32
        ).reshape(-1, k, sensors)

    for c in range(chunks):
        sends(c, start)
    for c in range(min(LOOK, chunks)):
        relays(c, start, True)
    forwards(0, start, True)
    for c in range(chunks):
        if c + LOOK < chunks:
            relays(c + LOOK, start, True)
        if c + 1 < chunks:
            forwards(c + 1, start, True)
        take(c, 0)
        if c < m:
            words(c)
        own[c].wait()
        weights[c].wait()

        @pl.when(busy)
        def _(c=c):
            for r in range(n // tile):
                image = image_of(x[c, r * tile:(r + 1) * tile], c)
                if c == 0:
                    acc[r * tile:(r + 1) * tile] = image
                else:
                    acc[r * tile:(r + 1) * tile] += image

    def lag_part(step):
        return pltpu.make_async_remote_copy(
            src_ref=acc.at[step], dst_ref=part.at[me],
            send_sem=red_out.at[step], recv_sem=red_in.at[me],
            device_id={"tm": lax.rem(me + step, n)}, device_id_type=MESH,
        )

    def lag_parts(near, act):
        for step in range(n - 1, 0, -1):
            @pl.when((me + step < n) & (straight(step // 2, chip) == near))
            def _(step=step):
                act(lag_part(step))

    lag_parts(True, start)
    for turn in range(chunks, m):
        words(turn)

    far_forwards(0, start, True)
    for c in range(chunks):
        if c + 1 < chunks:
            far_forwards(c + 1, start, True)
        take(c, 1)

        def far_images(step, c=c):
            r = lax.rem(row + 1 + lax.div(step, max(1, cols - 1)), rows)
            q = lax.rem(col + 1 + lax.rem(step, max(1, cols - 1)), cols)
            source = r * cols + q

            @pl.when(need(2 * source, chip))
            def _():
                image = image_of(far[c, pl.ds(2 * source, 2)], c)
                if c == 0:
                    acc[pl.ds(2 * source, 2)] = image
                else:
                    acc[pl.ds(2 * source, 2)] += image

        each(0, (rows - 1) * (cols - 1), far_images)

    lag_parts(False, start)

    def add_lag(lag, value):
        pltpu.make_async_remote_copy(
            src_ref=acc.at[0], dst_ref=part.at[lag],
            send_sem=red_out.at[0], recv_sem=red_in.at[lag],
            device_id={"tm": pair}, device_id_type=MESH,
        ).wait_recv()
        return value + part[lag]

    value = lax.fori_loop(0, me, add_lag, acc[0])
    for j in range(m):
        total[j] = value[:, j * share_size:(j + 1) * share_size]

    def to_floor(step):
        other = lax.rem(floor + step, m)
        return pltpu.make_async_remote_copy(
            src_ref=total.at[other], dst_ref=share.at[floor],
            send_sem=floor_out.at[step], recv_sem=floor_in.at[floor],
            device_id={"floor": other}, device_id_type=MESH,
        )

    for step in range(m - 1, 0, -1):
        to_floor(step).start()
    for c in range(chunks):
        sends(c, wait_send)
        relays(c, wait_send, False)
        forwards(c, wait_send, False)
        far_forwards(c, wait_send, False)

    lag_parts(True, wait_send)
    lag_parts(False, wait_send)
    result = total[floor]
    for step in range(1, m):
        source = lax.rem(floor + step, m)
        pltpu.make_async_remote_copy(
            src_ref=total.at[source], dst_ref=share.at[source],
            send_sem=floor_out.at[step], recv_sem=floor_in.at[source],
            device_id={"floor": source}, device_id_type=MESH,
        ).wait_recv()
        result = result + share[source]
    out_ref[0] = result.astype(out_ref.dtype)

    for step in range(1, m):
        to_floor(step).wait_send()


def solution(mesh):
    n, m = mesh.shape["tm"], mesh.shape["floor"]

    def local(samples, operator):
        _, k, depth = samples.shape
        sensors = operator.shape[1]
        chunks = 4
        width = depth // chunks
        return pl.pallas_call(
            functools.partial(kernel, n, m, chunks),
            out_shape=jax.ShapeDtypeStruct((1, k, sensors // m), jnp.bfloat16),
            in_specs=[pl.BlockSpec(memory_space=pl.ANY)] * 2,
            out_specs=pl.BlockSpec(memory_space=pltpu.VMEM),
            scratch_shapes=[
                pltpu.VMEM((chunks, n, k, width), jnp.bfloat16),
                pltpu.VMEM((chunks, n, k, width), jnp.bfloat16),
                pltpu.VMEM((chunks, sensors, width), jnp.bfloat16),
                pltpu.VMEM((n, k, sensors), jnp.float32),
                pltpu.VMEM((n, k, sensors), jnp.float32),
                pltpu.VMEM((m, k, sensors // m), jnp.float32),
                pltpu.VMEM((m, k, sensors // m), jnp.float32),
                pltpu.SemaphoreType.DMA((chunks,)),
                pltpu.SemaphoreType.DMA((chunks,)),
                pltpu.SemaphoreType.DMA((chunks, n // 2)),
                pltpu.SemaphoreType.DMA((chunks,)),
                pltpu.SemaphoreType.DMA((chunks, n // 2)),
                pltpu.SemaphoreType.DMA((chunks, n // 2, max(1, max(grid_of(n // 2)) - 1))),
                pltpu.SemaphoreType.DMA((chunks, n)),
                pltpu.SemaphoreType.DMA((n,)),
                pltpu.SemaphoreType.DMA((n,)),
                pltpu.SemaphoreType.DMA((m,)),
                pltpu.SemaphoreType.DMA((m,)),
                pltpu.SemaphoreType.REGULAR,
                pltpu.SemaphoreType.REGULAR,
            ],
            compiler_params=pltpu.CompilerParams(collective_id=0, has_side_effects=True),
        )(samples, operator)

    placed = (P("tm", None, "floor"), P("tm", None, "floor"))
    return jax.shard_map(
        local, mesh=mesh, in_specs=placed, out_specs=P("tm", None, "floor"), check_vma=False
    )
```
